256 devices in a mesh: dp: 32 (over y, x, core), mp: 8 (over z).
Axes of the slice: x: 4, y: 4, z: 8, core: 2. Of those that a mesh axis runs over, the one named last changes fastest.
Arguments:
- users_list: int32 [256, 256], P(('dp', 'mp')), may hold values from 0 to 4095, as said below
- items_list: int32 [256, 256], P(('dp', 'mp')), may hold values from 0 to 4095, as said below
- days_list: int32 [256, 32], P(('dp', 'mp')), may hold values from 0 to 1023, as said below
- status: int32 [256, 32, 256, 256], P(('dp', 'mp')), may hold values from 0 to 2
- user_factor: float32 [4096, 256], P('dp', 'mp'), may hold values from -2.4 to 2.4
- user_first: float32 [4096, 256], P('dp', 'mp'), may hold values from -6 to 6
- user_second: float32 [4096, 256], P('dp', 'mp'), may hold values from 0.05 to 2
- item_factor: float32 [4096, 256], P('dp', 'mp'), may hold values from -2.4 to 2.4
- item_first: float32 [4096, 256], P('dp', 'mp'), may hold values from -6 to 6
- item_second: float32 [4096, 256], P('dp', 'mp'), may hold values from 0.05 to 2
- day_factor: float32 [1024, 256], P('dp', 'mp'), may hold values from -2.4 to 2.4
- day_first: float32 [1024, 256], P('dp', 'mp'), may hold values from -6 to 6
- day_second: float32 [1024, 256], P('dp', 'mp'), may hold values from 1 to 3000
Outputs:
- new_user_factor: float32 [4096, 256], P('dp', 'mp')
- new_user_first: float32 [4096, 256], P('dp', 'mp')
- new_user_second: float32 [4096, 256], P('dp', 'mp')
- new_item_factor: float32 [4096, 256], P('dp', 'mp')
- new_item_first: float32 [4096, 256], P('dp', 'mp')
- new_item_second: float32 [4096, 256], P('dp', 'mp')
- new_day_factor: float32 [1024, 256], P('dp', 'mp')
- new_day_first: float32 [1024, 256], P('dp', 'mp')
- new_day_second: float32 [1024, 256], P('dp', 'mp')
The draws below stay inside these ranges and needn't reach their ends.
Inputs may be any that keep to these rules, and one draw needn't show every extreme that they name: `users_list`: the 256 users of a block are distinct; at most 12 of them lie in the rows n * 128 to (n + 1) * 128 - 1 of one index n of dp, and one such index holds exactly 12 users of every block. `items_list`: the 256 items of a block are distinct; at most 12 of them lie in the rows n * 128 to (n + 1) * 128 - 1 of one index n of dp, and one such index holds exactly 12 items of every block. `days_list`: the 32 days of a block are distinct; at most 2 of them lie in the rows n * 32 to (n + 1) * 32 - 1 of one index n of dp, and one such index holds exactly 2 days of every block.
All inputs are finite; a program needn't handle non-finite values.
Results may differ from the reference program's by a relative error of at most 0.0044.
Values may be sent and summed in bfloat16 or wider, within the bound.
A program may use at most 64 MiB of HBM per device.

```python
import math
import jax
import jax.numpy as jnp
from jax import lax

R = 256
BU = 256
BI = 256
BD = 32
UO = 128
IO = 128
DAYS_OWN = 32
BLOCKS = 256
NU = 4096
NI = 4096
ND = 1024
CAP_U = 12
CAP_I = 12
CAP_D = 2


def block_rows(base_key, blocks, row_count, locally_kept_lines, line_bundles, place_limit):
    subkeys = jax.random.split(base_key, 4)
    hot_owner = jax.random.randint(subkeys[0], (1, 1), 0, line_bundles)
    spare_slots = (line_bundles - 1) * place_limit
    ordering = jax.vmap(lambda subkey: jax.random.permutation(subkey, spare_slots))(jax.random.split(subkeys[1], blocks))
    chosen = ordering[:, :row_count - place_limit]
    owners = jnp.concatenate([jnp.broadcast_to(hot_owner, (blocks, place_limit)), (hot_owner + 1 + chosen // place_limit) % line_bundles], axis=1)
    slot_numbers = jnp.concatenate([jnp.broadcast_to(jnp.arange(place_limit)[None, :], (blocks, place_limit)), chosen % place_limit], axis=1)
    row_picks = jax.vmap(lambda subkey: jax.random.permutation(subkey, locally_kept_lines)[:place_limit])(jax.random.split(subkeys[2], blocks * line_bundles))
    row_picks = row_picks.reshape(blocks, line_bundles * place_limit)
    local_rows = jnp.take_along_axis(row_picks, owners * place_limit + slot_numbers, axis=1)
    global_rows = owners * locally_kept_lines + local_rows
    shuffle = jax.vmap(lambda subkey: jax.random.permutation(subkey, row_count))(jax.random.split(subkeys[3], blocks))
    return jnp.take_along_axis(global_rows, shuffle, axis=1).astype(jnp.int32)


def draw_users_list(key, part):
    return block_rows(jax.random.fold_in(key, 11), BLOCKS, BU, UO, NU // UO, CAP_U)


def draw_items_list(key, part):
    return block_rows(jax.random.fold_in(key, 22), BLOCKS, BI, IO, NI // IO, CAP_I)


def draw_days_list(key, part):
    return block_rows(jax.random.fold_in(key, 33), BLOCKS, BD, DAYS_OWN, ND // DAYS_OWN, CAP_D)


def place_ends(array, rng, low, high):
    index_at = [jax.random.randint(jax.random.fold_in(rng, axis), (), 0, length) for axis, length in enumerate(array.shape)]
    longest = array.shape.index(max(array.shape))
    next_to = index_at[:longest] + [(index_at[longest] + 1) % array.shape[longest]] + index_at[longest + 1:]
    return array.at[tuple(index_at)].set(low).at[tuple(next_to)].set(high)


def levels(key, extent, cuts, least, top_value):
    level = 1.0
    for dim, parts in cuts:
        steps = jax.random.uniform(jax.random.fold_in(jax.random.fold_in(key, 6), dim), (parts,), jnp.float32, least / len(cuts), top_value / len(cuts))
        level = level * jnp.repeat(jnp.exp(steps), extent[dim] // parts).reshape((-1,) + (1,) * (len(extent) - 1 - dim))
    return level


def normal_values(stream_key, dims, spread, limit, pieces=(), held_as=jnp.bfloat16):
    factor_of = levels(stream_key, dims, pieces, -0.22, 0.18) if pieces else 1.0
    result = jax.random.normal(stream_key, dims, jnp.float32) * spread * factor_of
    return jnp.minimum(jnp.maximum(result, -limit), limit).astype(held_as)


def setup_inputs(seed: int = 0) -> dict:
    splits = jax.random.split(jax.random.key(seed), 14)
    users_list = draw_users_list(jax.random.fold_in(splits[13], 71), 0)
    items_list = draw_items_list(jax.random.fold_in(splits[13], 71), 0)
    days_list = draw_days_list(jax.random.fold_in(splits[13], 71), 0)
    status = place_ends(jax.random.randint(splits[3], (BLOCKS, BD, BU, BI), 0, 3), jax.random.fold_in(splits[3], 1), 0, 2).astype(jnp.int32)
    user_factor = normal_values(splits[4], (NU, R), 0.4, 2.4, ((0, 32), (1, 8)), jnp.float32)
    user_first = normal_values(splits[5], (NU, R), 1.0, 6.0, ((0, 32), (1, 8)), jnp.float32)
    user_second = jnp.clip(jnp.exp(math.log(2.0) - 3.6888794 * jax.random.uniform(splits[6], (NU, R), jnp.float32) ** levels(splits[6], (NU, R), ((0, 32), (1, 8)), -0.2, 0.2)), 0.05, 2.0)
    item_factor = normal_values(splits[7], (NI, R), 0.4, 2.4, ((0, 32), (1, 8)), jnp.float32)
    item_first = normal_values(splits[8], (NI, R), 1.0, 6.0, ((0, 32), (1, 8)), jnp.float32)
    item_second = jnp.clip(jnp.exp(math.log(2.0) - 3.6888794 * jax.random.uniform(splits[9], (NI, R), jnp.float32) ** levels(splits[9], (NI, R), ((0, 32), (1, 8)), -0.2, 0.2)), 0.05, 2.0)
    day_factor = normal_values(splits[10], (ND, R), 0.4, 2.4, ((0, 32), (1, 8)), jnp.float32)
    day_first = normal_values(splits[11], (ND, R), 1.0, 6.0, ((0, 32), (1, 8)), jnp.float32)
    day_second = jnp.clip(jnp.exp(math.log(3000.0) - 8.006368 * jax.random.uniform(splits[12], (ND, R), jnp.float32) ** levels(splits[12], (ND, R), ((0, 32), (1, 8)), -0.2, 0.2)), 1.0, 3000.0)
    return {"users_list": users_list, "items_list": items_list, "days_list": days_list, "status": status, "user_factor": user_factor, "user_first": user_first, "user_second": user_second, "item_factor": item_factor, "item_first": item_first, "item_second": item_second, "day_factor": day_factor, "day_first": day_first, "day_second": day_second}


beta_one = 0.9
beta_two = 0.99
bias_one = 1.0 - 0.9 ** 10
bias_two = 1.0 - 0.99 ** 10
learn_rate = 0.01
epsilon = 1e-08
loss_scale = 0.0625
zero_weight = 2.0

def block_grads(user_row_values, item_row_values, day_row_values, block_status):
    day_count = day_row_values.shape[0]
    user_count = user_row_values.shape[0]
    scaled = day_row_values[:, None, :] * user_row_values[None, :, :]
    scaled_flat = scaled.reshape(day_count * user_count, -1)
    scaled_wide = scaled_flat.astype(jnp.float32)
    items_wide = item_row_values.astype(jnp.float32)
    logits = jnp.einsum('nr,ir->ni', scaled_wide, items_wide)
    chance = jax.nn.sigmoid(logits)
    status_flat = block_status.reshape(day_count * user_count, -1)
    residual = loss_scale * (jnp.where(status_flat == 1, chance - 1.0, 0.0) + jnp.where(status_flat == 2, zero_weight * chance, 0.0))
    residual = residual.astype(jnp.bfloat16)
    residual_wide = residual.astype(jnp.float32)
    projected = jnp.einsum('ni,ir->nr', residual_wide, items_wide).reshape(day_count, user_count, -1)
    user_gradient = lax.optimization_barrier(jnp.sum(projected * day_row_values[:, None, :].astype(jnp.float32), axis=0))
    day_gradient = lax.optimization_barrier(jnp.sum(projected * user_row_values[None, :, :].astype(jnp.float32), axis=1))
    item_gradient = jnp.einsum('ni,nr->ir', residual_wide, scaled_wide)
    return (user_gradient, item_gradient, day_gradient)

def adam_update(factor, first, second, gradient):
    first_new = beta_one * first + (1.0 - beta_one) * gradient
    second_new = beta_two * second + (1.0 - beta_two) * gradient * gradient
    change = learn_rate * (first_new / bias_one) / (jnp.sqrt(second_new / bias_two) + epsilon)
    return (factor - change, first_new, second_new)

def reference(users_list, items_list, days_list, status, user_factor, user_first, user_second, item_factor, item_first, item_second, day_factor, day_first, day_second):
    user_row_values = user_factor.astype(jnp.bfloat16)
    item_row_values = item_factor.astype(jnp.bfloat16)
    day_row_values = day_factor.astype(jnp.bfloat16)

    def one_block(carry, inputs):
        user_gradient_sum, item_gradient_sum, day_gradient_sum = carry
        user_index, item_index, day_index, block_status = inputs
        user_gradient, item_gradient, day_gradient = block_grads(user_row_values[user_index], item_row_values[item_index], day_row_values[day_index], block_status)
        return ((user_gradient_sum.at[user_index].add(user_gradient), item_gradient_sum.at[item_index].add(item_gradient), day_gradient_sum.at[day_index].add(day_gradient)), None)
    initial = (jnp.zeros(user_factor.shape, jnp.float32), jnp.zeros(item_factor.shape, jnp.float32), jnp.zeros(day_factor.shape, jnp.float32))
    totals, _ = lax.scan(one_block, initial, (users_list, items_list, days_list, status))
    user_gradient_sum, item_gradient_sum, day_gradient_sum = totals
    new_user_factor, new_user_first, new_user_second = adam_update(user_factor, user_first, user_second, user_gradient_sum)
    new_item_factor, new_item_first, new_item_second = adam_update(item_factor, item_first, item_second, item_gradient_sum)
    new_day_factor, new_day_first, new_day_second = adam_update(day_factor, day_first, day_second, day_gradient_sum)
    return (new_user_factor, new_user_first, new_user_second, new_item_factor, new_item_first, new_item_second, new_day_factor, new_day_first, new_day_second)
```

```python
import functools

import jax
import jax.numpy as jnp
from jax import lax
from jax.experimental import pallas as pl
from jax.experimental.pallas import tpu as pltpu
from jax.sharding import PartitionSpec as P

MESH = pl.DeviceIdType.MESH
F32, BF16, I32 = jnp.float32, jnp.bfloat16, jnp.int32

beta_one = 0.9
beta_two = 0.99
bias_one = 1.0 - 0.9**10
bias_two = 1.0 - 0.99**10
learn_rate = 0.01
epsilon = 1e-08

SLOTS = 16
DAY_SLOT = 12
DAY_BASE = 128
ROWS = 384
CHUNKS = 4


def iota(shape, dim):
    return lax.broadcasted_iota(I32, shape, dim)


def onehot(hit):
    return jnp.where(hit, 1.0, 0.0).astype(BF16)


def dot(a, b):
    return jnp.dot(a, b, preferred_element_type=F32)


def dot_nt(a, b):
    return lax.dot_general(a, b, (((1,), (1,)), ((), ())), preferred_element_type=F32)


def list_layout(rows_wanted, per_owner, owners, base, first_slot):
    n = rows_wanted.shape[1]
    owner = rows_wanted // per_owner
    code = (rows_wanted - owner * per_owner + base + 1).astype(F32)
    hit = owner == iota((owners, n), 0)
    before = onehot(iota((n, n), 0) < iota((n, n), 1))
    rank = dot(onehot(hit), before)
    slot = jnp.sum(jnp.where(hit, rank, 0.0), axis=0, keepdims=True).astype(I32) + first_slot
    coded = jnp.where(hit, code, 0.0).astype(BF16)
    return coded, slot, owner * SLOTS


def step_kernel(
    owners,
    peers,
    users_ref,
    items_ref,
    days_ref,
    status_hbm,
    user_ref,
    item_ref,
    day_ref,
    grad_ref,
    status_ref,
    list_out,
    list_in,
    table,
    row_out,
    row_in,
    slope_out,
    slope_in,
    part_out,
    part_in,
    serve_ud,
    serve_it,
    user_rows,
    user_rows_t,
    item_rows,
    item_half,
    day_rows,
    user_acc,
    item_acc,
    day_acc,
    status_sem,
    send_sem,
    recv_sem,
):
    me_d = lax.axis_index("dp")
    me_m = lax.axis_index("mp")
    tall = owners * SLOTS
    days_here = status_ref.shape[0]
    per_chunk = days_here // CHUNKS

    def status_copy(chunk):
        part = pl.ds(chunk * per_chunk, per_chunk)
        return pltpu.make_async_copy(
            status_hbm.at[0, part], status_ref.at[part], status_sem.at[chunk]
        )

    for chunk in range(CHUNKS):
        status_copy(chunk).start()

    barrier = pltpu.get_barrier_semaphore()

    @pl.loop(1, owners)
    def _(delta):
        pl.semaphore_signal(
            barrier, inc=1, device_id=(lax.rem(me_d + delta, owners), me_m), device_id_type=MESH
        )

    @pl.loop(1, peers)
    def _(delta):
        pl.semaphore_signal(
            barrier, inc=1, device_id=(me_d, lax.rem(me_m + delta, peers)), device_id_type=MESH
        )

    def plane_copy(source, landing, phase, delta):
        target = lax.rem(me_d + delta, owners)
        return pltpu.make_async_remote_copy(
            src_ref=source.at[target],
            dst_ref=landing.at[me_d],
            send_sem=send_sem.at[phase],
            recv_sem=recv_sem.at[phase],
            device_id=(target, me_m),
            device_id_type=MESH,
        )

    def plane_send(source, landing, phase):
        @pl.loop(1, owners)
        def _(delta):
            plane_copy(source, landing, phase, delta).start()

        landing[pl.ds(me_d, 1)] = source[pl.ds(me_d, 1)]

    def wait_all(buffer, count, sem):
        held = buffer.at[pl.ds(0, count)]
        pltpu.make_async_copy(held, held, sem).wait()

    u_coded, u_slot, u_first = list_layout(users_ref[...], 128, owners, 0, 0)
    i_coded, i_slot, i_first = list_layout(items_ref[...], 128, owners, 0, SLOTS)
    d_coded, d_slot, d_first = list_layout(days_ref[...], 32, owners, DAY_BASE, DAY_SLOT)
    lists = jnp.zeros((owners, 128), F32)
    for coded, slot in ((u_coded, u_slot), (i_coded, i_slot), (d_coded, d_slot)):
        lists = lists + dot_nt(coded, onehot(slot == iota((128, slot.shape[1]), 0)))
    for owner in range(owners):
        list_out[owner] = lists[owner : owner + 1, :]
    day_t = day_ref[...].T
    table[pl.ds(me_m, 1), :, 0:128] = user_ref[...].astype(BF16)[None]
    table[pl.ds(me_m, 1), :, 128:256] = jnp.zeros((1, 32, 128), BF16)
    table[pl.ds(me_m, 1), :, 128:160] = day_t.astype(BF16)[None]
    table[pl.ds(me_m, 1), :, 256:384] = item_ref[...].astype(BF16)[None]

    pl.semaphore_wait(barrier, owners + peers - 2)

    def table_copy(delta):
        return pltpu.make_async_remote_copy(
            src_ref=table.at[me_m],
            dst_ref=table.at[me_m],
            send_sem=send_sem.at[3],
            recv_sem=recv_sem.at[3],
            device_id=(me_d, lax.rem(me_m + delta, peers)),
            device_id_type=MESH,
        )

    @pl.loop(1, peers)
    def _(delta):
        table_copy(delta).start()

    plane_send(list_out, list_in, 0)

    u_target = u_first + u_slot
    i_target = i_first + i_slot - SLOTS
    d_target = d_first + d_slot

    def column(target):
        n = target.shape[1]
        return jnp.broadcast_to(target.astype(F32), (8, n)).T[:, 0:1].astype(I32)

    u_pick = onehot(column(u_target) == iota((u_target.shape[1], tall), 1))
    i_pick = onehot(column(i_target) == iota((i_target.shape[1], tall), 1))
    d_pick = onehot(column(d_target) == iota((d_target.shape[1], tall), 1))

    wait_all(list_in, owners - 1, recv_sem.at[0])
    wanted = jnp.concatenate([list_in[b] for b in range(owners)], axis=0)
    wanted_t = wanted.T.astype(I32) - 1
    for b in range(owners):
        rows = slice(b * SLOTS, (b + 1) * SLOTS)
        serve_ud[rows, :] = onehot(wanted_t[0:SLOTS, b : b + 1] == iota((SLOTS, 256), 1))
        serve_it[rows, :] = onehot(wanted_t[SLOTS : 2 * SLOTS, b : b + 1] == iota((SLOTS, 128), 1))

    wait_all(table, peers - 1, recv_sem.at[3])
    full = table[...].reshape(-1, ROWS)
    row_out[:, 0:SLOTS, :] = dot_nt(serve_ud[...], full[:, 0:256]).astype(BF16).reshape(owners, SLOTS, -1)
    row_out[:, SLOTS:, :] = dot_nt(serve_it[...], full[:, 256:384]).astype(BF16).reshape(owners, SLOTS, -1)
    plane_send(row_out, row_in, 1)

    serve_ud_t = serve_ud[...].astype(F32).T.astype(BF16)
    serve_it_t = serve_it[...].astype(F32).T.astype(BF16)
    wait_all(row_in, owners - 1, recv_sem.at[1])

    arrived_ud = row_in[:, 0:SLOTS, :].reshape(tall, -1)
    arrived_it = row_in[:, SLOTS:, :].reshape(tall, -1)
    users_f = dot(u_pick, arrived_ud)
    items_f = dot(i_pick, arrived_it)
    user_rows[...] = users_f.astype(BF16)
    user_rows_t[...] = users_f.T.astype(BF16)
    item_rows[...] = items_f.astype(BF16)
    item_half[...] = (0.5 * items_f).astype(BF16)
    day_rows[...] = dot(d_pick, arrived_ud)
    user_acc[...] = jnp.zeros_like(user_acc)
    item_acc[...] = jnp.zeros_like(item_acc)

    @pl.loop(0, CHUNKS)
    def _(chunk):
        status_copy(chunk).wait()
        first = pl.multiple_of(chunk * per_chunk, per_chunk)
        rows = day_rows[pl.ds(first, per_chunk), :]
        users = user_rows[...]
        users_wide = users.astype(F32)
        users_t = user_rows_t[...]
        items = item_rows[...]
        half = item_half[...]
        slopes = []
        spread = []
        sums = []
        for k in range(per_chunk):
            row = rows[k : k + 1, :]
            logits = dot_nt(users * row.astype(BF16), half)
            kind = status_ref[first + k].astype(F32)
            slope = (kind * (jnp.tanh(logits) + (2.0 * kind - 3.0))).astype(BF16)
            projected = dot(slope, items)
            user_acc[...] += projected * row
            sums.append(jnp.sum(projected * users_wide, axis=0, keepdims=True))
            slopes.append(slope)
            spread.append(users_t * jnp.broadcast_to(row, (8, row.shape[1])).T[:, 0:1].astype(BF16))
        day_acc[pl.ds(first, per_chunk), :] = jnp.concatenate(sums, axis=0)
        item_acc[...] += dot(jnp.concatenate(spread, axis=1), jnp.concatenate(slopes, axis=0))

    u_place = onehot(u_target == iota((tall, u_target.shape[1]), 0))
    i_place = onehot(i_target == iota((tall, i_target.shape[1]), 0))
    d_place = onehot(d_target == iota((tall, d_target.shape[1]), 0))
    placed = dot(u_place, user_acc[...].astype(BF16)) + dot(d_place, day_acc[...].astype(BF16))
    slope_out[:, 0:SLOTS, :] = placed.astype(BF16).reshape(owners, SLOTS, -1)
    placed = dot_nt(i_place, item_acc[...].astype(BF16))
    slope_out[:, SLOTS:, :] = placed.astype(BF16).reshape(owners, SLOTS, -1)
    plane_send(slope_out, slope_in, 2)
    wait_all(slope_in, owners - 1, recv_sem.at[2])

    part_ud = dot(serve_ud_t, slope_in[:, 0:SLOTS, :].reshape(tall, -1))
    part_it = dot(serve_it_t, slope_in[:, SLOTS:, :].reshape(tall, -1))
    part_out[:, :, 0:256] = part_ud.T.astype(BF16).reshape(peers, -1, 256)
    part_out[:, :, 256:384] = part_it.T.astype(BF16).reshape(peers, -1, 128)

    def part_copy(delta):
        target = lax.rem(me_m + delta, peers)
        return pltpu.make_async_remote_copy(
            src_ref=part_out.at[target],
            dst_ref=part_in.at[me_m],
            send_sem=send_sem.at[4],
            recv_sem=recv_sem.at[4],
            device_id=(me_d, target),
            device_id_type=MESH,
        )

    @pl.loop(1, peers)
    def _(delta):
        part_copy(delta).start()

    part_in[pl.ds(me_m, 1)] = part_out[pl.ds(me_m, 1)]
    wait_all(part_in, peers - 1, recv_sem.at[4])
    total = part_in[0].astype(F32)
    for m in range(1, peers):
        total = total + part_in[m].astype(F32)
    grad_ref[...] = total * (1.0 / 32.0)

    wait_all(list_out, owners - 1, send_sem.at[0])
    wait_all(row_out, owners - 1, send_sem.at[1])
    wait_all(slope_out, owners - 1, send_sem.at[2])
    wait_all(table, peers - 1, send_sem.at[3])
    wait_all(part_out, peers - 1, send_sem.at[4])


def adam_kernel(grad_ref, *refs):
    arguments, results = refs[:9], refs[9:]
    grads = (
        grad_ref[:, 0:128],
        grad_ref[:, 256:384],
        grad_ref[:, 128:256].T[0:32, :],
    )
    for which, grad in enumerate(grads):
        factor, first, second = (ref[...] for ref in arguments[3 * which : 3 * which + 3])
        first_new = beta_one * first + (1.0 - beta_one) * grad
        second_new = beta_two * second + (1.0 - beta_two) * grad * grad
        change = learn_rate * (first_new / bias_one) / (jnp.sqrt(second_new / bias_two) + epsilon)
        results[3 * which][...] = factor - change
        results[3 * which + 1][...] = first_new
        results[3 * which + 2][...] = second_new


def local(
    users_list,
    items_list,
    days_list,
    status,
    user_factor,
    user_first,
    user_second,
    item_factor,
    item_first,
    item_second,
    day_factor,
    day_first,
    day_second,
):
    owners = lax.axis_size("dp")
    peers = lax.axis_size("mp")
    rank = user_factor.shape[1] * peers
    users, items, days = users_list.shape[1], items_list.shape[1], days_list.shape[1]
    own = user_factor.shape[1]
    tall = owners * SLOTS
    vmem = pl.BlockSpec(memory_space=pltpu.VMEM)
    grad = pl.pallas_call(
        functools.partial(step_kernel, owners, peers),
        out_shape=jax.ShapeDtypeStruct((own, ROWS), F32),
        in_specs=[vmem] * 3 + [pl.BlockSpec(memory_space=pl.ANY)] + [vmem] * 3,
        out_specs=vmem,
        scratch_shapes=[
            pltpu.VMEM(status.shape[1:], I32),
            pltpu.VMEM((owners, 1, 128), F32),
            pltpu.VMEM((owners, 1, 128), F32),
            pltpu.VMEM((peers, own, ROWS), BF16),
            pltpu.VMEM((owners, 2 * SLOTS, rank), BF16),
            pltpu.VMEM((owners, 2 * SLOTS, rank), BF16),
            pltpu.VMEM((owners, 2 * SLOTS, rank), BF16),
            pltpu.VMEM((owners, 2 * SLOTS, rank), BF16),
            pltpu.VMEM((peers, own, ROWS), BF16),
            pltpu.VMEM((peers, own, ROWS), BF16),
            pltpu.VMEM((tall, 256), BF16),
            pltpu.VMEM((tall, 128), BF16),
            pltpu.VMEM((users, rank), BF16),
            pltpu.VMEM((rank, users), BF16),
            pltpu.VMEM((items, rank), BF16),
            pltpu.VMEM((items, rank), BF16),
            pltpu.VMEM((days, rank), F32),
            pltpu.VMEM((users, rank), F32),
            pltpu.VMEM((rank, items), F32),
            pltpu.VMEM((days, rank), F32),
            pltpu.SemaphoreType.DMA((CHUNKS,)),
            pltpu.SemaphoreType.DMA((5,)),
            pltpu.SemaphoreType.DMA((5,)),
        ],
        compiler_params=pltpu.CompilerParams(
            collective_id=0, has_side_effects=True, vmem_limit_bytes=50 << 20
        ),
        name="step",
    )(users_list, items_list, days_list, status, user_factor.T, item_factor.T, day_factor)
    tables = [
        user_factor.T,
        user_first.T,
        user_second.T,
        item_factor.T,
        item_first.T,
        item_second.T,
        day_factor,
        day_first,
        day_second,
    ]
    new = pl.pallas_call(
        adam_kernel,
        out_shape=[jax.ShapeDtypeStruct(table.shape, F32) for table in tables],
        in_specs=[vmem] * 10,
        out_specs=[vmem] * 9,
        name="adam",
    )(grad, *tables)
    return tuple(x.T for x in new[:6]) + tuple(new[6:])


def solution(mesh):
    lists = P(("dp", "mp"), None)
    rows = P("dp", "mp")
    return jax.shard_map(
        local,
        mesh=mesh,
        in_specs=(lists,) * 3 + (P(("dp", "mp"), None, None, None),) + (rows,) * 9,
        out_specs=(rows,) * 9,
        check_vma=False,
    )
```

```python
import functools

import jax
import jax.numpy as jnp
from jax import lax
from jax.experimental import pallas as pl
from jax.experimental.pallas import tpu as pltpu
from jax.sharding import PartitionSpec as P

MESH = pl.DeviceIdType.MESH
F32, BF16, I32 = jnp.float32, jnp.bfloat16, jnp.int32

beta_one = 0.9
beta_two = 0.99
bias_one = 1.0 - 0.9**10
bias_two = 1.0 - 0.99**10
learn_rate = 0.01
epsilon = 1e-08

SLOTS = 16
DAY_SLOT = 12
DAY_BASE = 128
ROWS = 384
CHUNKS = 4

FAR_FIRST = sorted(
    ((y, x, c) for y in range(4) for x in range(4) for c in range(2) if y or x or c),
    key=lambda step: -(min(step[0], 4 - step[0]) + min(step[1], 4 - step[1])),
)
Z_FAR_FIRST = (4, 3, 5, 2, 6, 1, 7)


def iota(shape, dim):
    return lax.broadcasted_iota(I32, shape, dim)


def onehot(hit):
    return jnp.where(hit, 1.0, 0.0).astype(BF16)


def dot(a, b):
    return jnp.dot(a, b, preferred_element_type=F32)


def dot_nt(a, b):
    return lax.dot_general(a, b, (((1,), (1,)), ((), ())), preferred_element_type=F32)


def list_layout(rows_wanted, per_owner, owners, base, first_slot):
    n = rows_wanted.shape[1]
    owner = rows_wanted // per_owner
    code = (rows_wanted - owner * per_owner + base + 1).astype(F32)
    hit = owner == iota((owners, n), 0)
    before = onehot(iota((n, n), 0) < iota((n, n), 1))
    rank = dot(onehot(hit), before)
    slot = jnp.sum(jnp.where(hit, rank, 0.0), axis=0, keepdims=True).astype(I32) + first_slot
    coded = jnp.where(hit, code, 0.0).astype(BF16)
    return coded, slot, owner * SLOTS


def step_kernel(
    owners,
    peers,
    users_hbm,
    items_hbm,
    days_hbm,
    status_hbm,
    user_hbm,
    item_hbm,
    day_hbm,
    grad_ref,
    users_ref,
    items_ref,
    days_ref,
    user_ref,
    item_ref,
    day_ref,
    status_ref,
    list_out,
    list_in,
    table_ud,
    table_it,
    day_pack,
    day_full,
    rows_ud_out,
    rows_ud_in,
    rows_it_out,
    rows_it_in,
    slopes_ud_out,
    slopes_ud_in,
    slopes_it_out,
    slopes_it_in,
    part_ud_out,
    part_ud_in,
    part_it_out,
    part_it_in,
    serve_ud,
    serve_it,
    serve_ud_t,
    serve_it_t,
    user_rows,
    user_rows_t,
    item_rows,
    item_half,
    day_rows,
    slope_ref,
    user_acc,
    item_acc,
    day_acc,
    status_sem,
    load_sem,
    send_sem,
    recv_sem,
):
    me_d = lax.axis_index("dp")
    me_m = lax.axis_index("mp")
    tall = owners * SLOTS
    days_here = status_ref.shape[0]
    per_chunk = days_here // CHUNKS

    loads = [
        pltpu.make_async_copy(source, landing, load_sem.at[n])
        for n, (source, landing) in enumerate(
            (
                (users_hbm, users_ref),
                (items_hbm, items_ref),
                (days_hbm, days_ref),
                (user_hbm, user_ref),
                (day_hbm, day_ref),
                (item_hbm, item_ref),
            )
        )
    ]
    for load in loads:
        load.start()

    barrier = pltpu.get_barrier_semaphore()

    @pl.loop(1, owners)
    def _(delta):
        pl.semaphore_signal(
            barrier, inc=1, device_id=(lax.rem(me_d + delta, owners), me_m), device_id_type=MESH
        )

    @pl.loop(1, peers)
    def _(delta):
        pl.semaphore_signal(
            barrier, inc=1, device_id=(me_d, lax.rem(me_m + delta, peers)), device_id_type=MESH
        )

    def status_copy(chunk):
        part = pl.ds(chunk * per_chunk, per_chunk)
        return pltpu.make_async_copy(
            status_hbm.at[0, part], status_ref.at[part], status_sem.at[chunk]
        )

    for chunk in range(CHUNKS):
        status_copy(chunk).start()

    here_y, here_x, here_c = me_d // 8, lax.rem(me_d // 2, 4), lax.rem(me_d, 2)

    def plane_send(source, landing, phase):
        for dy, dx, dc in FAR_FIRST:
            y, x, c = lax.rem(here_y + dy, 4), lax.rem(here_x + dx, 4), lax.rem(here_c + dc, 2)
            target = y * 8 + x * 2 + c
            pltpu.make_async_remote_copy(
                src_ref=source.at[target],
                dst_ref=landing.at[me_d],
                send_sem=send_sem.at[phase],
                recv_sem=recv_sem.at[phase],
                device_id=(target, me_m),
                device_id_type=MESH,
            ).start()
        landing[pl.ds(me_d, 1)] = source[pl.ds(me_d, 1)]

    def column_gather(pieces, phase):
        for delta in Z_FAR_FIRST:
            pltpu.make_async_remote_copy(
                src_ref=pieces.at[me_m],
                dst_ref=pieces.at[me_m],
                send_sem=send_sem.at[phase],
                recv_sem=recv_sem.at[phase],
                device_id=(me_d, lax.rem(me_m + delta, peers)),
                device_id_type=MESH,
            ).start()

    def column_scatter(source, landing, phase):
        for delta in Z_FAR_FIRST:
            target = lax.rem(me_m + delta, peers)
            pltpu.make_async_remote_copy(
                src_ref=source.at[target],
                dst_ref=landing.at[me_m],
                send_sem=send_sem.at[phase],
                recv_sem=recv_sem.at[phase],
                device_id=(me_d, target),
                device_id_type=MESH,
            ).start()
        landing[pl.ds(me_m, 1)] = source[pl.ds(me_m, 1)]

    def wait_all(buffer, sem):
        held = buffer.at[pl.ds(0, buffer.shape[0] - 1)]
        pltpu.make_async_copy(held, held, sem).wait()

    for load in loads:
        load.wait()

    table_ud[pl.ds(me_m, 1), 0:32, :] = user_ref[...].astype(BF16)[None]
    table_it[pl.ds(me_m, 1), :, :] = item_ref[...].astype(BF16)[None]
    day_t = day_ref[...].T
    day_pack[...] = jnp.zeros_like(day_pack)
    day_pack[:, 0:32] = day_t[0:16, :]
    day_pack[:, 32:64] = day_t[16:32, :]
    table_ud[pl.ds(me_m, 1), 32:48, :] = day_pack[...].astype(BF16)[None]

    u_coded, u_slot, u_first = list_layout(users_ref[...], 128, owners, 0, 0)
    i_coded, i_slot, i_first = list_layout(items_ref[...], 128, owners, 0, SLOTS)
    d_coded, d_slot, d_first = list_layout(days_ref[...], 32, owners, DAY_BASE, DAY_SLOT)
    lists = jnp.zeros((owners, 128), F32)
    for coded, slot in ((u_coded, u_slot), (i_coded, i_slot), (d_coded, d_slot)):
        lists = lists + dot_nt(coded, onehot(slot == iota((128, slot.shape[1]), 0)))
    for owner in range(owners):
        list_out[owner] = lists[owner : owner + 1, :]

    pl.semaphore_wait(barrier, owners + peers - 2)

    column_gather(table_ud, 0)
    plane_send(list_out, list_in, 2)
    column_gather(table_it, 1)

    u_target = u_first + u_slot
    i_target = i_first + i_slot - SLOTS
    d_target = d_first + d_slot

    def column(target):
        n = target.shape[1]
        return jnp.broadcast_to(target.astype(F32), (8, n)).T[:, 0:1].astype(I32)

    u_pick = onehot(column(u_target) == iota((u_target.shape[1], tall), 1))
    i_pick = onehot(column(i_target) == iota((i_target.shape[1], tall), 1))
    d_pick = onehot(column(d_target) == iota((d_target.shape[1], tall), 1))

    wait_all(list_in, recv_sem.at[2])
    wanted = jnp.concatenate([list_in[b] for b in range(owners)], axis=0)
    wanted_t = wanted.T.astype(I32) - 1
    for b in range(owners):
        rows = slice(b * SLOTS, (b + 1) * SLOTS)
        serve_ud[rows, :] = onehot(wanted_t[0:SLOTS, b : b + 1] == iota((SLOTS, 256), 1))
        serve_it[rows, :] = onehot(wanted_t[SLOTS : 2 * SLOTS, b : b + 1] == iota((SLOTS, 128), 1))

    wait_all(table_ud, recv_sem.at[0])
    for m in range(peers):
        packed = table_ud[m, 32:48, :].astype(F32)
        lane = iota(packed.shape, 1)
        day_full[m, 0:16, :] = jnp.where(lane < 32, packed, 0.0).astype(BF16)
        day_full[m, 16:32, :] = jnp.where(lane < 32, pltpu.roll(packed, 96, 1), 0.0).astype(BF16)
    served = dot_nt(serve_ud[:, 0:128], table_ud[:, 0:32, :].reshape(-1, 128))
    served = served + dot_nt(serve_ud[:, 128:256], day_full[...].reshape(-1, 128))
    rows_ud_out[...] = served.astype(BF16).reshape(owners, SLOTS, -1)
    plane_send(rows_ud_out, rows_ud_in, 3)
    wait_all(table_it, recv_sem.at[1])
    served = dot_nt(serve_it[...], table_it[...].reshape(-1, 128))
    rows_it_out[...] = served.astype(BF16).reshape(owners, SLOTS, -1)
    plane_send(rows_it_out, rows_it_in, 4)

    serve_ud_t[...] = serve_ud[...].astype(F32).T.astype(BF16)
    serve_it_t[...] = serve_it[...].astype(F32).T.astype(BF16)
    user_acc[...] = jnp.zeros_like(user_acc)
    item_acc[...] = jnp.zeros_like(item_acc)
    for chunk in range(CHUNKS):
        status_copy(chunk).wait()

    wait_all(rows_ud_in, recv_sem.at[3])
    arrived = rows_ud_in[...].reshape(tall, -1)
    users_f = dot(u_pick, arrived)
    user_rows[...] = users_f.astype(BF16)
    user_rows_t[...] = users_f.T.astype(BF16)
    day_rows[...] = dot(d_pick, arrived)
    wait_all(rows_it_in, recv_sem.at[4])
    items_f = dot(i_pick, rows_it_in[...].reshape(tall, -1))
    item_rows[...] = items_f.astype(BF16)
    item_half[...] = (0.5 * items_f).astype(BF16)

    @pl.loop(0, CHUNKS)
    def _(chunk):
        first = pl.multiple_of(chunk * per_chunk, per_chunk)
        rows = day_rows[pl.ds(first, per_chunk), :]
        users = user_rows[...]
        users_t = user_rows_t[...]
        half = item_half[...]
        slopes = []
        spread = []
        for k in range(per_chunk):
            row = rows[k : k + 1, :]
            logits = dot_nt(users * row.astype(BF16), half)
            kind = status_ref[first + k].astype(F32)
            slope = (kind * (jnp.tanh(logits) + (2.0 * kind - 3.0))).astype(BF16)
            slope_ref[first + k] = slope
            slopes.append(slope)
            spread.append(users_t * jnp.broadcast_to(row, (8, row.shape[1])).T[:, 0:1].astype(BF16))
        item_acc[...] += dot(jnp.concatenate(spread, axis=1), jnp.concatenate(slopes, axis=0))

    i_place = onehot(i_target == iota((tall, i_target.shape[1]), 0))
    placed = dot_nt(i_place, item_acc[...].astype(BF16))
    slopes_it_out[...] = placed.astype(BF16).reshape(owners, SLOTS, -1)
    plane_send(slopes_it_out, slopes_it_in, 5)

    @pl.loop(0, CHUNKS)
    def _(chunk):
        first = pl.multiple_of(chunk * per_chunk, per_chunk)
        rows = day_rows[pl.ds(first, per_chunk), :]
        users_wide = user_rows[...].astype(F32)
        items = item_rows[...]
        sums = []
        for k in range(per_chunk):
            projected = dot(slope_ref[first + k], items)
            user_acc[...] += projected * rows[k : k + 1, :]
            sums.append(jnp.sum(projected * users_wide, axis=0, keepdims=True))
        day_acc[pl.ds(first, per_chunk), :] = jnp.concatenate(sums, axis=0)

    u_place = onehot(u_target == iota((tall, u_target.shape[1]), 0))
    d_place = onehot(d_target == iota((tall, d_target.shape[1]), 0))
    placed = dot(u_place, user_acc[...].astype(BF16)) + dot(d_place, day_acc[...].astype(BF16))
    slopes_ud_out[...] = placed.astype(BF16).reshape(owners, SLOTS, -1)
    plane_send(slopes_ud_out, slopes_ud_in, 6)

    wait_all(slopes_it_in, recv_sem.at[5])
    part = dot(serve_it_t[...], slopes_it_in[...].reshape(tall, -1))
    part_it_out[...] = part.T.astype(BF16).reshape(peers, -1, 128)
    column_scatter(part_it_out, part_it_in, 7)

    wait_all(slopes_ud_in, recv_sem.at[6])
    part = dot(serve_ud_t[...], slopes_ud_in[...].reshape(tall, -1))
    part_ud_out[:, 0:32, :] = part[0:128, :].T.astype(BF16).reshape(peers, -1, 128)
    day_part = part[128:256, :].T.reshape(peers, 2, 16, 128)
    for m in range(peers):
        part_ud_out[m, 32:48, :] = (day_part[m, 0] + pltpu.roll(day_part[m, 1], 32, 1)).astype(BF16)
    column_scatter(part_ud_out, part_ud_in, 8)

    wait_all(part_it_in, recv_sem.at[7])
    total = part_it_in[0].astype(F32)
    for m in range(1, peers):
        total = total + part_it_in[m].astype(F32)
    grad_ref[:, 256:384] = total * (1.0 / 32.0)
    wait_all(part_ud_in, recv_sem.at[8])
    total = part_ud_in[0].astype(F32)
    for m in range(1, peers):
        total = total + part_ud_in[m].astype(F32)
    total = total * (1.0 / 32.0)
    grad_ref[:, 0:128] = total[0:32, :]
    grad_ref[0:16, 128:256] = total[32:48, :]
    grad_ref[16:32, 128:256] = pltpu.roll(total[32:48, :], 96, 1)

    for phase, buffer in enumerate(
        (
            table_ud,
            table_it,
            list_out,
            rows_ud_out,
            rows_it_out,
            slopes_it_out,
            slopes_ud_out,
            part_it_out,
            part_ud_out,
        )
    ):
        wait_all(buffer, send_sem.at[phase])


def adam_kernel(grad_ref, *refs):
    tables, results, held, made, load_sem, store_sem = (
        refs[:9],
        refs[9:18],
        refs[18:27],
        refs[27:36],
        refs[36],
        refs[37],
    )
    loads = [pltpu.make_async_copy(tables[n], held[n], load_sem.at[n]) for n in range(9)]
    stores = [pltpu.make_async_copy(made[n], results[n], store_sem.at[n]) for n in range(9)]
    for load in loads:
        load.start()
    grads = (
        grad_ref[:, 0:128],
        grad_ref[:, 256:384],
        grad_ref[:, 128:256].T[0:32, :],
    )
    for which, grad in enumerate(grads):
        picked = slice(3 * which, 3 * which + 3)
        for load in loads[picked]:
            load.wait()
        factor, first, second = (ref[...] for ref in held[picked])
        first_new = beta_one * first + (1.0 - beta_one) * grad
        second_new = beta_two * second + (1.0 - beta_two) * grad * grad
        change = learn_rate * (first_new / bias_one) / (jnp.sqrt(second_new / bias_two) + epsilon)
        for ref, value in zip(made[picked], (factor - change, first_new, second_new)):
            ref[...] = value
        for store in stores[picked]:
            store.start()
    for store in stores:
        store.wait()


def local(
    users_list,
    items_list,
    days_list,
    status,
    user_factor,
    user_first,
    user_second,
    item_factor,
    item_first,
    item_second,
    day_factor,
    day_first,
    day_second,
):
    owners = lax.axis_size("dp")
    peers = lax.axis_size("mp")
    rank = user_factor.shape[1] * peers
    users, items, days = users_list.shape[1], items_list.shape[1], days_list.shape[1]
    own = user_factor.shape[1]
    tall = owners * SLOTS
    vmem = pl.BlockSpec(memory_space=pltpu.VMEM)
    hbm = pl.BlockSpec(memory_space=pltpu.HBM)
    slots = pltpu.VMEM((owners, SLOTS, rank), BF16)
    grad = pl.pallas_call(
        functools.partial(step_kernel, owners, peers),
        out_shape=jax.ShapeDtypeStruct((own, ROWS), F32),
        in_specs=[hbm] * 7,
        out_specs=vmem,
        scratch_shapes=[
            pltpu.VMEM(users_list.shape, I32),
            pltpu.VMEM(items_list.shape, I32),
            pltpu.VMEM(days_list.shape, I32),
            pltpu.VMEM((own, user_factor.shape[0]), F32),
            pltpu.VMEM((own, item_factor.shape[0]), F32),
            pltpu.VMEM(day_factor.shape, F32),
            pltpu.VMEM(status.shape[1:], I32),
            pltpu.VMEM((owners, 1, 128), F32),
            pltpu.VMEM((owners, 1, 128), F32),
            pltpu.VMEM((peers, 48, 128), BF16),
            pltpu.VMEM((peers, 32, 128), BF16),
            pltpu.VMEM((16, 128), F32),
            pltpu.VMEM((peers, 32, 128), BF16),
            *[slots] * 8,
            pltpu.VMEM((peers, 48, 128), BF16),
            pltpu.VMEM((peers, 48, 128), BF16),
            pltpu.VMEM((peers, 32, 128), BF16),
            pltpu.VMEM((peers, 32, 128), BF16),
            pltpu.VMEM((tall, 256), BF16),
            pltpu.VMEM((tall, 128), BF16),
            pltpu.VMEM((256, tall), BF16),
            pltpu.VMEM((128, tall), BF16),
            pltpu.VMEM((users, rank), BF16),
            pltpu.VMEM((rank, users), BF16),
            pltpu.VMEM((items, rank), BF16),
            pltpu.VMEM((items, rank), BF16),
            pltpu.VMEM((days, rank), F32),
            pltpu.VMEM((days, users, items), BF16),
            pltpu.VMEM((users, rank), F32),
            pltpu.VMEM((rank, items), F32),
            pltpu.VMEM((days, rank), F32),
            pltpu.SemaphoreType.DMA((CHUNKS,)),
            pltpu.SemaphoreType.DMA((6,)),
            pltpu.SemaphoreType.DMA((9,)),
            pltpu.SemaphoreType.DMA((9,)),
        ],
        compiler_params=pltpu.CompilerParams(
            collective_id=0, has_side_effects=True, vmem_limit_bytes=60 << 20
        ),
        name="step",
    )(users_list, items_list, days_list, status, user_factor.T, item_factor.T, day_factor)
    tables = [
        user_factor.T,
        user_first.T,
        user_second.T,
        item_factor.T,
        item_first.T,
        item_second.T,
        day_factor,
        day_first,
        day_second,
    ]
    new = pl.pallas_call(
        adam_kernel,
        out_shape=[jax.ShapeDtypeStruct(table.shape, F32) for table in tables],
        in_specs=[vmem] + [hbm] * 9,
        out_specs=[hbm] * 9,
        scratch_shapes=[pltpu.VMEM(table.shape, F32) for table in tables] * 2
        + [pltpu.SemaphoreType.DMA((9,))] * 2,
        compiler_params=pltpu.CompilerParams(vmem_limit_bytes=8 << 20),
        name="adam",
    )(grad, *tables)
    return tuple(x.T for x in new[:6]) + tuple(new[6:])


def solution(mesh):
    lists = P(("dp", "mp"), None)
    rows = P("dp", "mp")
    return jax.shard_map(
        local,
        mesh=mesh,
        in_specs=(lists,) * 3 + (P(("dp", "mp"), None, None, None),) + (rows,) * 9,
        out_specs=(rows,) * 9,
        check_vma=False,
    )
```

```python
import functools

import jax
import jax.numpy as jnp
from jax import lax
from jax.experimental import pallas as pl
from jax.experimental.pallas import tpu as pltpu
from jax.sharding import PartitionSpec as P

MESH = pl.DeviceIdType.MESH
F32, BF16, I32 = jnp.float32, jnp.bfloat16, jnp.int32

beta_one = 0.9
beta_two = 0.99
bias_one = 1.0 - 0.9**10
bias_two = 1.0 - 0.99**10
learn_rate = 0.01
epsilon = 1e-08

SLOTS = 16
DAY_SLOT = 12
DAY_BASE = 128
ROWS = 384
CHUNKS = 4

FAR_FIRST = sorted(
    ((y, x, c) for y in range(4) for x in range(4) for c in range(2) if y or x or c),
    key=lambda step: -(min(step[0], 4 - step[0]) + min(step[1], 4 - step[1])),
)
Z_FAR_FIRST = (4, 3, 5, 2, 6, 1, 7)


def iota(shape, dim):
    return lax.broadcasted_iota(I32, shape, dim)


def onehot(hit):
    return jnp.where(hit, 1.0, 0.0).astype(BF16)


def dot(a, b):
    return jnp.dot(a, b, preferred_element_type=F32)


def dot_nt(a, b):
    return lax.dot_general(a, b, (((1,), (1,)), ((), ())), preferred_element_type=F32)


def list_layout(rows_wanted, per_owner, owners, base, first_slot):
    n = rows_wanted.shape[1]
    owner = rows_wanted // per_owner
    code = (rows_wanted - owner * per_owner + base + 1).astype(F32)
    hit = owner == iota((owners, n), 0)
    before = onehot(iota((n, n), 0) < iota((n, n), 1))
    rank = dot(onehot(hit), before)
    slot = jnp.sum(jnp.where(hit, rank, 0.0), axis=0, keepdims=True).astype(I32) + first_slot
    coded = jnp.where(hit, code, 0.0).astype(BF16)
    return coded, slot, owner * SLOTS


def step_kernel(
    owners,
    peers,
    users_hbm,
    items_hbm,
    days_hbm,
    status_hbm,
    user_hbm,
    item_hbm,
    day_hbm,
    grad_ref,
    users_ref,
    items_ref,
    days_ref,
    user_ref,
    item_ref,
    day_ref,
    status_ref,
    list_out,
    list_in,
    table_ud,
    table_it,
    day_pack,
    day_full,
    rows_ud_out,
    rows_ud_in,
    rows_it_out,
    rows_it_in,
    slopes_ud_out,
    slopes_ud_in,
    slopes_it_out,
    slopes_it_in,
    part_ud_out,
    part_ud_in,
    part_it_out,
    part_it_in,
    serve_ud,
    serve_it,
    serve_ud_t,
    serve_it_t,
    user_rows,
    spread,
    item_rows,
    item_half,
    day_rows,
    slope_ref,
    user_acc,
    item_acc,
    day_acc,
    status_sem,
    load_sem,
    send_sem,
    recv_sem,
):
    me_d = lax.axis_index("dp")
    me_m = lax.axis_index("mp")
    loads = [
        pltpu.make_async_copy(source, landing, load_sem.at[n])
        for n, (source, landing) in enumerate(
            (
                (users_hbm, users_ref),
                (items_hbm, items_ref),
                (days_hbm, days_ref),
                (user_hbm, user_ref),
                (day_hbm, day_ref),
                (item_hbm, item_ref),
            )
        )
    ]
    for load in loads:
        load.start()
    tall = owners * SLOTS
    days_here, users_count, items_count = status_ref.shape
    per_chunk = days_here // CHUNKS

    barrier = pltpu.get_barrier_semaphore()

    @pl.loop(1, owners)
    def _(delta):
        pl.semaphore_signal(
            barrier, inc=1, device_id=(lax.rem(me_d + delta, owners), me_m), device_id_type=MESH
        )

    @pl.loop(1, peers)
    def _(delta):
        pl.semaphore_signal(
            barrier, inc=1, device_id=(me_d, lax.rem(me_m + delta, peers)), device_id_type=MESH
        )

    def status_copy(chunk):
        part = pl.ds(chunk * per_chunk, per_chunk)
        return pltpu.make_async_copy(
            status_hbm.at[0, part], status_ref.at[part], status_sem.at[chunk]
        )

    for chunk in range(CHUNKS):
        status_copy(chunk).start()

    here_y, here_x, here_c = me_d // 8, lax.rem(me_d // 2, 4), lax.rem(me_d, 2)

    def plane_send(source, landing, phase):
        for dy, dx, dc in FAR_FIRST:
            y, x, c = lax.rem(here_y + dy, 4), lax.rem(here_x + dx, 4), lax.rem(here_c + dc, 2)
            target = y * 8 + x * 2 + c
            pltpu.make_async_remote_copy(
                src_ref=source.at[target],
                dst_ref=landing.at[me_d],
                send_sem=send_sem.at[phase],
                recv_sem=recv_sem.at[phase],
                device_id=(target, me_m),
                device_id_type=MESH,
            ).start()
        landing[pl.ds(me_d, 1)] = source[pl.ds(me_d, 1)]

    def column_gather(pieces, phase):
        for delta in Z_FAR_FIRST:
            pltpu.make_async_remote_copy(
                src_ref=pieces.at[me_m],
                dst_ref=pieces.at[me_m],
                send_sem=send_sem.at[phase],
                recv_sem=recv_sem.at[phase],
                device_id=(me_d, lax.rem(me_m + delta, peers)),
                device_id_type=MESH,
            ).start()

    def column_scatter(source, landing, phase):
        for delta in Z_FAR_FIRST:
            target = lax.rem(me_m + delta, peers)
            pltpu.make_async_remote_copy(
                src_ref=source.at[target],
                dst_ref=landing.at[me_m],
                send_sem=send_sem.at[phase],
                recv_sem=recv_sem.at[phase],
                device_id=(me_d, target),
                device_id_type=MESH,
            ).start()
        landing[pl.ds(me_m, 1)] = source[pl.ds(me_m, 1)]

    def wait_all(buffer, sem):
        held = buffer.at[pl.ds(0, buffer.shape[0] - 1)]
        pltpu.make_async_copy(held, held, sem).wait()

    for load in loads:
        load.wait()

    table_ud[pl.ds(me_m, 1), 0:32, :] = user_ref[...].astype(BF16)[None]
    day_t = day_ref[...].T
    for q in range(4):
        day_pack[:, 32 * q : 32 * q + 32] = day_t[8 * q : 8 * q + 8, :]
    table_ud[pl.ds(me_m, 1), 32:40, :] = day_pack[...].astype(BF16)[None]
    table_it[pl.ds(me_m, 1), :, :] = item_ref[...].astype(BF16)[None]

    pl.semaphore_wait(barrier, owners + peers - 2)
    column_gather(table_ud, 0)

    u_coded, u_slot, u_first = list_layout(users_ref[...], 128, owners, 0, 0)
    i_coded, i_slot, i_first = list_layout(items_ref[...], 128, owners, 0, SLOTS)
    d_coded, d_slot, d_first = list_layout(days_ref[...], 32, owners, DAY_BASE, DAY_SLOT)
    lists = jnp.zeros((owners, 128), F32)
    for coded, slot in ((u_coded, u_slot), (i_coded, i_slot), (d_coded, d_slot)):
        lists = lists + dot_nt(coded, onehot(slot == iota((128, slot.shape[1]), 0)))
    for owner in range(owners):
        list_out[owner] = lists[owner : owner + 1, :]

    plane_send(list_out, list_in, 2)
    column_gather(table_it, 1)

    u_target = u_first + u_slot
    i_target = i_first + i_slot - SLOTS
    d_target = d_first + d_slot

    def column(target):
        n = target.shape[1]
        return jnp.broadcast_to(target.astype(F32), (8, n)).T[:, 0:1].astype(I32)

    u_pick = onehot(column(u_target) == iota((u_target.shape[1], tall), 1))
    i_pick = onehot(column(i_target) == iota((i_target.shape[1], tall), 1))
    d_pick = onehot(column(d_target) == iota((d_target.shape[1], tall), 1))

    wait_all(list_in, recv_sem.at[2])
    wanted = jnp.concatenate([list_in[b] for b in range(owners)], axis=0)
    wanted_t = wanted.T.astype(I32) - 1
    for b in range(owners):
        rows = slice(b * SLOTS, (b + 1) * SLOTS)
        serve_ud[rows, :] = onehot(wanted_t[0:SLOTS, b : b + 1] == iota((SLOTS, 256), 1))
        serve_it[rows, :] = onehot(wanted_t[SLOTS : 2 * SLOTS, b : b + 1] == iota((SLOTS, 128), 1))

    wait_all(table_ud, recv_sem.at[0])
    packed = table_ud[:, 32:40, :].astype(F32).reshape(-1, 128)
    lane = iota(packed.shape, 1)
    for q in range(4):
        turned = packed if q == 0 else pltpu.roll(packed, 128 - 32 * q, 1)
        day_full[:, 8 * q : 8 * q + 8, :] = jnp.where(lane < 32, turned, 0.0).reshape(-1, 8, 128)
    served = dot_nt(serve_ud[:, 0:128], table_ud[:, 0:32, :].reshape(-1, 128))
    served = served + dot_nt(serve_ud[:, 128:256], day_full[...].astype(BF16).reshape(-1, 128))
    rows_ud_out[...] = served.astype(BF16).reshape(owners, SLOTS, -1)
    plane_send(rows_ud_out, rows_ud_in, 3)
    wait_all(table_it, recv_sem.at[1])
    served = dot_nt(serve_it[...], table_it[...].reshape(-1, 128))
    rows_it_out[...] = served.astype(BF16).reshape(owners, SLOTS, -1)
    plane_send(rows_it_out, rows_it_in, 4)

    serve_ud_t[...] = serve_ud[...].astype(F32).T.astype(BF16)
    serve_it_t[...] = serve_it[...].astype(F32).T.astype(BF16)
    user_acc[...] = jnp.zeros_like(user_acc)
    item_acc[...] = jnp.zeros_like(item_acc)
    for chunk in range(CHUNKS):
        status_copy(chunk).wait()

    wait_all(rows_ud_in, recv_sem.at[3])
    arrived = rows_ud_in[...].reshape(tall, -1)
    users_f = dot(u_pick, arrived)
    user_rows[...] = users_f.astype(BF16)
    day_rows[...] = dot(d_pick, arrived)
    rows_t = day_rows[...].T
    users_t = users_f.T.astype(BF16)
    for k in range(days_here):
        spread[:, k * users_count : (k + 1) * users_count] = users_t * rows_t[:, k : k + 1].astype(BF16)
    wait_all(rows_it_in, recv_sem.at[4])
    items_f = dot(i_pick, rows_it_in[...].reshape(tall, -1))
    item_rows[...] = items_f.astype(BF16)
    item_half[...] = (0.5 * items_f).astype(BF16)

    def make_slopes(chunk):
        users = user_rows[...]
        half = item_half[...]
        for k in range(chunk * per_chunk, (chunk + 1) * per_chunk):
            logits = dot_nt(users * day_rows[k : k + 1, :].astype(BF16), half)
            kind = status_ref[k].astype(F32)
            slope_ref[k] = (kind * (jnp.tanh(logits) + (2.0 * kind - 3.0))).astype(BF16)

    def chunk_slopes(chunk):
        return slope_ref[chunk * per_chunk : (chunk + 1) * per_chunk].reshape(-1, items_count)

    def add_items(chunk):
        width = per_chunk * users_count
        item_acc[...] += dot(spread[:, chunk * width : (chunk + 1) * width], chunk_slopes(chunk))

    make_slopes(0)
    for chunk in range(1, CHUNKS):
        add_items(chunk - 1)
        make_slopes(chunk)
    add_items(CHUNKS - 1)

    i_place = onehot(i_target == iota((tall, i_target.shape[1]), 0))
    placed = dot_nt(i_place, item_acc[...].astype(BF16))
    slopes_it_out[...] = placed.astype(BF16).reshape(owners, SLOTS, -1)
    plane_send(slopes_it_out, slopes_it_in, 5)

    users_wide = user_rows[...].astype(F32)
    items = item_rows[...]
    for chunk in range(CHUNKS):
        projected = dot(chunk_slopes(chunk), items)
        acc = user_acc[...]
        sums = []
        for n in range(per_chunk):
            k = chunk * per_chunk + n
            part = projected[n * users_count : (n + 1) * users_count]
            acc = acc + part * day_rows[k : k + 1, :]
            sums.append(jnp.sum(part * users_wide, axis=0, keepdims=True))
        user_acc[...] = acc
        day_acc[chunk * per_chunk : (chunk + 1) * per_chunk, :] = jnp.concatenate(sums, axis=0)

    u_place = onehot(u_target == iota((tall, u_target.shape[1]), 0))
    d_place = onehot(d_target == iota((tall, d_target.shape[1]), 0))
    placed = dot(u_place, user_acc[...].astype(BF16)) + dot(d_place, day_acc[...].astype(BF16))
    slopes_ud_out[...] = placed.astype(BF16).reshape(owners, SLOTS, -1)
    plane_send(slopes_ud_out, slopes_ud_in, 6)

    wait_all(slopes_it_in, recv_sem.at[5])
    part = dot(serve_it_t[...], slopes_it_in[...].reshape(tall, -1))
    part_it_out[...] = part.T.astype(BF16).reshape(peers, -1, 128)
    column_scatter(part_it_out, part_it_in, 7)

    wait_all(slopes_ud_in, recv_sem.at[6])
    part = dot(serve_ud_t[...], slopes_ud_in[...].reshape(tall, -1))
    part_ud_out[:, 0:32, :] = part[0:128, :].T.astype(BF16).reshape(peers, -1, 128)
    day_part = part[128:256, :].T.reshape(peers, 4, 8, 128)
    packed = day_part[:, 0].reshape(-1, 128)
    for q in range(1, 4):
        packed = packed + pltpu.roll(day_part[:, q].reshape(-1, 128), 32 * q, 1)
    part_ud_out[:, 32:40, :] = packed.astype(BF16).reshape(peers, 8, 128)
    column_scatter(part_ud_out, part_ud_in, 8)

    wait_all(part_it_in, recv_sem.at[7])
    total = part_it_in[0].astype(F32)
    for m in range(1, peers):
        total = total + part_it_in[m].astype(F32)
    grad_ref[:, 256:384] = total * (1.0 / 32.0)
    wait_all(part_ud_in, recv_sem.at[8])
    total = part_ud_in[0].astype(F32)
    for m in range(1, peers):
        total = total + part_ud_in[m].astype(F32)
    total = total * (1.0 / 32.0)
    grad_ref[:, 0:128] = total[0:32, :]
    packed = total[32:40, :]
    grad_ref[0:8, 128:256] = packed
    for q in range(1, 4):
        grad_ref[8 * q : 8 * q + 8, 128:256] = pltpu.roll(packed, 128 - 32 * q, 1)

    for phase, buffer in enumerate(
        (
            table_ud,
            table_it,
            list_out,
            rows_ud_out,
            rows_it_out,
            slopes_it_out,
            slopes_ud_out,
            part_it_out,
            part_ud_out,
        )
    ):
        wait_all(buffer, send_sem.at[phase])


def adam_kernel(grad_ref, *refs):
    tables, results, held, made, load_sem, store_sem = (
        refs[:9],
        refs[9:18],
        refs[18:27],
        refs[27:36],
        refs[36],
        refs[37],
    )
    loads = [pltpu.make_async_copy(tables[n], held[n], load_sem.at[n]) for n in range(9)]
    stores = [pltpu.make_async_copy(made[n], results[n], store_sem.at[n]) for n in range(9)]
    for load in loads:
        load.start()
    grads = (
        grad_ref[:, 0:128],
        grad_ref[:, 256:384],
        grad_ref[:, 128:256].T[0:32, :],
    )
    for which, grad in enumerate(grads):
        picked = slice(3 * which, 3 * which + 3)
        for load in loads[picked]:
            load.wait()
        factor, first, second = (ref[...] for ref in held[picked])
        first_new = beta_one * first + (1.0 - beta_one) * grad
        second_new = beta_two * second + (1.0 - beta_two) * grad * grad
        change = learn_rate * (first_new / bias_one) / (jnp.sqrt(second_new / bias_two) + epsilon)
        for ref, value in zip(made[picked], (factor - change, first_new, second_new)):
            ref[...] = value
        for store in stores[picked]:
            store.start()
    for store in stores:
        store.wait()


def local(
    users_list,
    items_list,
    days_list,
    status,
    user_factor,
    user_first,
    user_second,
    item_factor,
    item_first,
    item_second,
    day_factor,
    day_first,
    day_second,
):
    owners = lax.axis_size("dp")
    peers = lax.axis_size("mp")
    rank = user_factor.shape[1] * peers
    users, items, days = users_list.shape[1], items_list.shape[1], days_list.shape[1]
    own = user_factor.shape[1]
    tall = owners * SLOTS
    vmem = pl.BlockSpec(memory_space=pltpu.VMEM)
    hbm = pl.BlockSpec(memory_space=pltpu.HBM)
    slots = pltpu.VMEM((owners, SLOTS, rank), BF16)
    grad = pl.pallas_call(
        functools.partial(step_kernel, owners, peers),
        out_shape=jax.ShapeDtypeStruct((own, ROWS), F32),
        in_specs=[hbm] * 7,
        out_specs=vmem,
        scratch_shapes=[
            pltpu.VMEM(users_list.shape, I32),
            pltpu.VMEM(items_list.shape, I32),
            pltpu.VMEM(days_list.shape, I32),
            pltpu.VMEM((own, user_factor.shape[0]), F32),
            pltpu.VMEM((own, item_factor.shape[0]), F32),
            pltpu.VMEM(day_factor.shape, F32),
            pltpu.VMEM(status.shape[1:], I32),
            pltpu.VMEM((owners, 1, 128), F32),
            pltpu.VMEM((owners, 1, 128), F32),
            pltpu.VMEM((peers, 40, 128), BF16),
            pltpu.VMEM((peers, 32, 128), BF16),
            pltpu.VMEM((8, 128), F32),
            pltpu.VMEM((peers, 32, 128), F32),
            *[slots] * 8,
            pltpu.VMEM((peers, 40, 128), BF16),
            pltpu.VMEM((peers, 40, 128), BF16),
            pltpu.VMEM((peers, 32, 128), BF16),
            pltpu.VMEM((peers, 32, 128), BF16),
            pltpu.VMEM((tall, 256), BF16),
            pltpu.VMEM((tall, 128), BF16),
            pltpu.VMEM((256, tall), BF16),
            pltpu.VMEM((128, tall), BF16),
            pltpu.VMEM((users, rank), BF16),
            pltpu.VMEM((rank, days * users), BF16),
            pltpu.VMEM((items, rank), BF16),
            pltpu.VMEM((items, rank), BF16),
            pltpu.VMEM((days, rank), F32),
            pltpu.VMEM((days, users, items), BF16),
            pltpu.VMEM((users, rank), F32),
            pltpu.VMEM((rank, items), F32),
            pltpu.VMEM((days, rank), F32),
            pltpu.SemaphoreType.DMA((CHUNKS,)),
            pltpu.SemaphoreType.DMA((6,)),
            pltpu.SemaphoreType.DMA((9,)),
            pltpu.SemaphoreType.DMA((9,)),
        ],
        compiler_params=pltpu.CompilerParams(
            collective_id=0, has_side_effects=True, vmem_limit_bytes=60 << 20
        ),
        name="step",
    )(users_list, items_list, days_list, status, user_factor.T, item_factor.T, day_factor)
    tables = [
        user_factor.T,
        user_first.T,
        user_second.T,
        item_factor.T,
        item_first.T,
        item_second.T,
        day_factor,
        day_first,
        day_second,
    ]
    new = pl.pallas_call(
        adam_kernel,
        out_shape=[jax.ShapeDtypeStruct(table.shape, F32) for table in tables],
        in_specs=[vmem] + [hbm] * 9,
        out_specs=[hbm] * 9,
        scratch_shapes=[pltpu.VMEM(table.shape, F32) for table in tables] * 2
        + [pltpu.SemaphoreType.DMA((9,))] * 2,
        compiler_params=pltpu.CompilerParams(vmem_limit_bytes=8 << 20),
        name="adam",
    )(grad, *tables)
    return tuple(x.T for x in new[:6]) + tuple(new[6:])


def solution(mesh):
    lists = P(("dp", "mp"), None)
    rows = P("dp", "mp")
    return jax.shard_map(
        local,
        mesh=mesh,
        in_specs=(lists,) * 3 + (P(("dp", "mp"), None, None, None),) + (rows,) * 9,
        out_specs=(rows,) * 9,
        check_vma=False,
    )
```
